32 devices in a mesh: dp: 8 (over z, core), sp: 4 (over y, x).
Axes of the slice: x: 2, y: 2, z: 4, core: 2. Of those that a mesh axis runs over, the one named last changes fastest.
Arguments:
- gate_pre: bfloat16 [2048, 8192], P('dp', 'sp'), may hold values from -6 to 6
- up_pre: bfloat16 [2048, 8192], P('dp', 'sp'), may hold values from -6 to 6
- w_down: bfloat16 [8192, 6144], P('sp'), may hold values from -0.0625 to 0.0625
- route_logits: float32 [4096, 2], P(('dp', 'sp')), may hold values from -8 to 8
- expert_ids: int32 [4096, 2], P(('dp', 'sp')), may hold values from 0 to 7, as said below
- d_out: bfloat16 [4096, 6144], P(('dp', 'sp')), may hold values from -6 to 6
Outputs:
- mixed: bfloat16 [4096, 6144], P(('dp', 'sp'))
- logit_grads: float32 [4096, 2], P(('dp', 'sp'))
- gate_grads: bfloat16 [2048, 8192], P('dp', 'sp')
- up_grads: bfloat16 [2048, 8192], P('dp', 'sp')
- down_grads: float32 [8192, 6144], P('sp', 'dp')
The draws below stay inside these ranges and needn't reach their ends.
Inputs may be any that keep to these rules, and one draw needn't show every extreme that they name: `expert_ids`: each row names two different experts. Of the 128 rows of one device, a quarter of 64 up to 64 name expert 0, and exactly 64 on some device in every draw.
All inputs are finite; a program needn't handle non-finite values.
Results may differ from the reference program's by a relative error of at most 0.022.
Values may be sent and summed in bfloat16 or wider, within the bound.
A program may use at most 128 MiB of HBM per device.

```python
import jax
import jax.numpy as jnp
from jax import lax

D = 6144
TOPK = 2
HID = 8192
TOK_DEV = 128
SLOT_DEV = 64
SLOTS = 256
TOKENS = 4096
N_DP = 8
N_SP = 4


def draw_expert_ids(key, part):
    blocks_all = TOKENS // TOK_DEV
    key_count = jax.random.fold_in(key, 11)
    key_full = jax.random.fold_in(key, 12)
    key_order = jax.random.fold_in(key, 13)
    key_other = jax.random.fold_in(key, 14)
    key_first = jax.random.fold_in(key, 15)
    key_step = jax.random.fold_in(key, 16)
    key_swap = jax.random.fold_in(key, 17)
    loads = jax.random.randint(key_count, (blocks_all,), SLOT_DEV // 4, SLOT_DEV + 1)
    full_block = jax.random.randint(key_full, (), 0, blocks_all)
    loads = jnp.where(jnp.arange(blocks_all) == full_block, SLOT_DEV, loads)
    order_keys = jax.random.split(key_order, blocks_all)
    ranks = jax.vmap(lambda one_key: jax.random.permutation(one_key, TOK_DEV))(order_keys)
    chosen = (ranks < loads[:, None]).reshape(TOKENS)
    other = jax.random.randint(key_other, (TOKENS,), 1, 8)
    first = jax.random.randint(key_first, (TOKENS,), 1, 8)
    second = 1 + (first - 1 + jax.random.randint(key_step, (TOKENS,), 1, 7)) % 7
    column_a = jnp.where(chosen, 0, first)
    column_b = jnp.where(chosen, other, second)
    swapped = jax.random.randint(key_swap, (TOKENS,), 0, 2) == 1
    left = jnp.where(swapped, column_b, column_a)
    right = jnp.where(swapped, column_a, column_b)
    return jnp.stack([left, right], axis=1).astype(jnp.int32)


def raised(entries, stream_key, source, target, parts, factor):
    def block_of(position):
        return (jnp.arange(entries.shape[position]) // (entries.shape[position] // parts)).reshape((-1,) + (1,) * (entries.ndim - 1 - position))

    one_side = jax.random.permutation(stream_key, parts)[block_of(target)]
    other_side = (block_of(target) + parts // 2) % parts
    return jnp.where((block_of(source) == one_side) | (block_of(source) == other_side), factor * entries, entries)


def steps_of(key, extent, shards, low, high):
    gain, own = 1.0, jax.random.fold_in(key, 6)
    for dim, blocks in shards:
        steps = jnp.exp(jax.random.uniform(jax.random.fold_in(own, dim), (blocks,), jnp.float32, low / len(shards), high / len(shards)))
        gain = gain * jnp.repeat(steps, extent[dim] // blocks).reshape([-1 if axis == dim else 1 for axis in range(len(extent))])
    return gain


def scatter_about(own_key, shape, spread, bound, pieces=(), held_as=jnp.bfloat16):
    entries = spread * jax.random.normal(own_key, shape, jnp.float32)
    if pieces:
        entries = entries * steps_of(own_key, shape, pieces, -0.22, 0.18)
    return jnp.clip(entries, -bound, bound).astype(held_as)


def heavy_noise(rng, dims, deviation, bound, shards, heavy, held_as=jnp.bfloat16):
    entries = deviation * jax.random.normal(rng, dims, jnp.float32)
    if shards:
        entries = entries * steps_of(rng, dims, shards, -0.22, 0.18)
    return jnp.clip(raised(entries, jax.random.fold_in(rng, 3), *heavy), -bound, bound).astype(held_as)


def setup_inputs(seed: int = 0) -> dict:
    seeds = jax.random.split(jax.random.key(seed), 7)
    return {
        "gate_pre": scatter_about(seeds[0], (SLOTS * N_DP, HID), 1.0, 6.0, ((0, 8), (1, 4))),
        "up_pre": scatter_about(seeds[1], (SLOTS * N_DP, HID), 1.0, 6.0, ((0, 8), (1, 4))),
        "w_down": scatter_about(seeds[2], (HID, D), HID ** -0.5, 0.0625, ((0, 4),)),
        "route_logits": scatter_about(seeds[3], (TOKENS, TOPK), 2.0, 8.0, ((0, 32),), jnp.float32),
        "expert_ids": draw_expert_ids(jax.random.fold_in(seeds[6], 71), 0),
        "d_out": heavy_noise(seeds[5], (TOKENS, D), 1.0, 6.0, ((0, 32),), (0, 1, 32, 2.75)),
    }


def reference(gate_pre, up_pre, w_down, route_logits, expert_ids, d_out):
    cycle_tokens = TOK_DEV * N_SP
    local_width = HID // N_SP

    def cycle_pass(grad_total, inputs):
        gate_cycle, up_cycle, logit_cycle, expert_cycle, cot_cycle = inputs
        gate_wide = gate_cycle.astype(jnp.float32)
        up_wide = up_cycle.astype(jnp.float32)
        sigma_gate = jax.nn.sigmoid(gate_wide)
        silu_gate = gate_wide * sigma_gate
        hidden = (silu_gate * up_wide).astype(jnp.bfloat16)
        routed = jnp.any(expert_cycle == 0, axis=1)
        routed_int = routed.astype(jnp.int32)
        slot_rank = (jnp.cumsum(routed_int.reshape(N_SP, TOK_DEV), axis=1) - 1).reshape(cycle_tokens).astype(jnp.int32)
        owner = jnp.arange(cycle_tokens, dtype=jnp.int32) // TOK_DEV
        slot_index = (owner * SLOT_DEV + slot_rank).astype(jnp.int32)
        expert_out = jnp.zeros((SLOTS, D), jnp.float32)
        for member in range(N_SP):
            lower = member * local_width
            partial_out = jnp.dot(hidden[:, lower:lower + local_width], w_down[lower:lower + local_width], preferred_element_type=jnp.float32)
            expert_out = expert_out + lax.optimization_barrier(partial_out.astype(jnp.bfloat16)).astype(jnp.float32)
        routed_float = routed.astype(jnp.float32)
        token_out = expert_out[jnp.where(routed, slot_index, 0)] * routed_float[:, None]
        first_zero = expert_cycle[:, 0] == 0
        own_logit = jnp.where(first_zero, logit_cycle[:, 0], logit_cycle[:, 1])
        other_logit = jnp.where(first_zero, logit_cycle[:, 1], logit_cycle[:, 0])
        weight_zero = routed_float * jax.nn.sigmoid(own_logit - other_logit)
        mixed = (weight_zero[:, None] * token_out).astype(jnp.bfloat16)
        weight_grad = jnp.sum(cot_cycle.astype(jnp.float32) * token_out, axis=1)
        logit_grad = weight_grad * weight_zero * (1.0 - weight_zero)
        first_col = jnp.where(first_zero, logit_grad, -logit_grad)
        logit_grads = jnp.stack([first_col, -first_col], axis=1)
        slot_cot = (weight_zero[:, None] * cot_cycle.astype(jnp.float32)).astype(jnp.bfloat16)
        target = jnp.where(routed, slot_index, SLOTS).astype(jnp.int32)
        d_expert = jnp.zeros((SLOTS, D), jnp.bfloat16).at[target].set(slot_cot, mode="drop")
        d_hidden = jnp.dot(d_expert, w_down.T, preferred_element_type=jnp.float32)
        gate_grads = (d_hidden * up_wide * sigma_gate * (1.0 + gate_wide * (1.0 - sigma_gate))).astype(jnp.bfloat16)
        up_grads = (d_hidden * silu_gate).astype(jnp.bfloat16)
        grad_total = grad_total + jnp.dot(hidden.T, d_expert, preferred_element_type=jnp.float32)
        return grad_total, (mixed, logit_grads, gate_grads, up_grads)

    inputs = (gate_pre.reshape(N_DP, SLOTS, HID), up_pre.reshape(N_DP, SLOTS, HID),
              route_logits.reshape(N_DP, cycle_tokens, TOPK), expert_ids.reshape(N_DP, cycle_tokens, TOPK),
              d_out.reshape(N_DP, cycle_tokens, D))
    down_grads, stacked = lax.scan(cycle_pass, jnp.zeros((HID, D), jnp.float32), inputs)
    mixed, logit_grads, gate_grads, up_grads = stacked
    return (mixed.reshape(TOKENS, D), logit_grads.reshape(TOKENS, TOPK),
            gate_grads.reshape(SLOTS * N_DP, HID), up_grads.reshape(SLOTS * N_DP, HID), down_grads)
```

```python
import functools

import jax
import jax.numpy as jnp
from jax import lax
from jax.experimental import pallas as pl
from jax.experimental.pallas import tpu as pltpu
from jax.sharding import PartitionSpec as P

MESH = pl.DeviceIdType.MESH


def exchange_kernel(
    n_dp, n_sp, hid_ref, dslot_ref, w_ref, rs_ref, dhid_ref, hall_ref, dall_ref,
    part, dcyc, wcol, wrow, wsem, local_sem,
    right_send, left_send, pair_send, hrecv, asend, arecv, gsend, grecv, bsend, brecv, rsend, rrecv,
):
    dp, sp = lax.axis_index("dp"), lax.axis_index("sp")
    chips = n_dp // 2
    chip, core = lax.div(dp, 2), lax.rem(dp, 2)
    slot_rows, width = dslot_ref.shape
    block = width // n_dp
    hid_width = hid_ref.shape[1]
    tn = wcol.shape[2]
    th = wrow.shape[1]
    n_col, n_row = width // tn, hid_width // th

    barrier = pltpu.get_barrier_semaphore()
    for off in range(1, n_dp):
        pl.semaphore_signal(barrier, inc=1, device_id={"dp": lax.rem(dp + off, n_dp)}, device_id_type=MESH)
    for off in range(1, n_sp):
        pl.semaphore_signal(barrier, inc=1, device_id={"sp": lax.rem(sp + off, n_sp)}, device_id_type=MESH)

    def col_load(step, slot):
        return pltpu.make_async_copy(
            w_ref.at[:, pl.ds(pl.multiple_of(step * tn, tn), tn)], wcol.at[slot], wsem.at[slot]
        )

    def row_load(step, slot):
        return pltpu.make_async_copy(
            w_ref.at[pl.ds(pl.multiple_of(step * th, th), th), :], wrow.at[slot], wsem.at[2 + slot]
        )

    col_load(0, 0).start()
    row_load(0, 0).start()
    pl.semaphore_wait(barrier, n_dp - 1 + n_sp - 1)

    def remote(src, dst, send, recv, **where):
        return pltpu.make_async_remote_copy(
            src_ref=src, dst_ref=dst, send_sem=send, recv_sem=recv, device_id=where, device_id_type=MESH
        )

    def a_send(off):
        other = lax.rem(dp + off, n_dp)
        return remote(
            dslot_ref.at[:, pl.ds(pl.multiple_of(other * block, block), block)], dall_ref.at[dp, sp],
            asend.at[off], arecv.at[dp], dp=other,
        )

    def a_wait(off):
        other = lax.rem(dp + off, n_dp)
        pltpu.make_async_copy(dall_ref.at[other, sp], dall_ref.at[other, sp], arecv.at[other]).wait()

    for off in range(1, n_dp):
        a_send(off).start()

    def h_block(index, src=None):
        return hall_ref.at[index]

    def h_send(index, src, to_chip, send):
        return remote(src, hall_ref.at[index], send, hrecv.at[index], dp=to_chip * 2 + core)

    def h_pair(index, src, send):
        return remote(src, hall_ref.at[index], send, hrecv.at[index], dp=chip * 2 + 1 - core)

    def h_wait(index):
        pltpu.make_async_copy(hall_ref.at[index], hall_ref.at[index], hrecv.at[index]).wait()

    @pl.when(chip + 1 < chips)
    def _():
        h_send(dp, hid_ref, chip + 1, right_send.at[0]).start()

    @pl.when(chip >= 1)
    def _():
        h_send(dp, hid_ref, chip - 1, left_send.at[0]).start()

    h_pair(dp, hid_ref, pair_send.at[chip]).start()

    def g_send(off):
        return remote(dslot_ref, dcyc.at[sp], gsend.at[off], grecv.at[sp], sp=lax.rem(sp + off, n_sp))

    for off in range(1, n_sp):
        g_send(off).start()

    own = [
        pltpu.make_async_copy(dslot_ref, dcyc.at[sp], local_sem.at[0]),
        pltpu.make_async_copy(
            dslot_ref.at[:, pl.ds(pl.multiple_of(dp * block, block), block)], dall_ref.at[dp, sp], local_sem.at[1]
        ),
        pltpu.make_async_copy(hid_ref, hall_ref.at[dp], local_sem.at[2]),
    ]
    for copy in own:
        copy.start()

    def r_send(step, off):
        other = lax.rem(sp + off, n_sp)
        cols = pl.ds(pl.multiple_of(step * tn, tn), tn)
        return remote(
            part.at[other, :, cols], rs_ref.at[sp, :, cols],
            rsend.at[step, off], rrecv.at[step, sp], sp=other,
        )

    def col_step(step, carry):
        slot = lax.rem(step, 2)

        @pl.when(step + 1 < n_col)
        def _():
            col_load(step + 1, 1 - slot).start()

        col_load(step, slot).wait()
        cols = pl.ds(pl.multiple_of(step * tn, tn), tn)
        product = jnp.dot(hid_ref[...], wcol[slot], preferred_element_type=jnp.float32)
        part[:, :, cols] = product.astype(jnp.bfloat16).reshape(n_sp, slot_rows, tn)
        for off in range(1, n_sp):
            r_send(step, off).start()
        return carry

    lax.fori_loop(0, n_col, col_step, 0)
    own_part = pltpu.make_async_copy(part.at[sp], rs_ref.at[sp], local_sem.at[3])
    own_part.start()

    for copy in own:
        copy.wait()
    for off in range(1, n_dp):
        a_wait(off)

    def b_send(off):
        return remote(dall_ref.at[:, sp], dall_ref.at[:, sp], bsend.at[off], brecv.at[sp], sp=lax.rem(sp + off, n_sp))

    for off in range(1, n_sp):
        b_send(off).start()

    def relay(step):
        @pl.when(chip - step >= 0)
        def _():
            index = (chip - step) * 2 + core
            h_wait(index)

            @pl.when(chip + 1 < chips)
            def _():
                h_send(index, h_block(index), chip + 1, right_send.at[step]).start()

            h_pair(index, h_block(index), pair_send.at[chip - step]).start()

        @pl.when(chip + step < chips)
        def _():
            index = (chip + step) * 2 + core
            h_wait(index)

            @pl.when(chip >= 1)
            def _():
                h_send(index, h_block(index), chip - 1, left_send.at[step]).start()

            h_pair(index, h_block(index), pair_send.at[chip + step]).start()

    relay(1)

    for off in range(1, n_sp):
        other = lax.rem(sp + off, n_sp)
        pltpu.make_async_copy(dcyc.at[other], dcyc.at[other], grecv.at[other]).wait()

    def row_step(step, carry):
        slot = lax.rem(step, 2)

        @pl.when(step + 1 < n_row)
        def _():
            row_load(step + 1, 1 - slot).start()

        row_load(step, slot).wait()
        dhid_ref[:, pl.ds(pl.multiple_of(step * th, th), th)] = lax.dot_general(
            dcyc[...].reshape(n_sp * slot_rows, width), wrow[slot], (((1,), (1,)), ((), ())),
            preferred_element_type=jnp.float32,
        )
        return carry

    lax.fori_loop(0, n_row, row_step, 0)

    for step in range(2, chips):
        relay(step)

    for index in range(chips):
        h_wait(index * 2 + 1 - core)
    for off in range(1, n_sp):
        other = lax.rem(sp + off, n_sp)
        pltpu.make_async_copy(dall_ref.at[:, other], dall_ref.at[:, other], brecv.at[other]).wait()

    def drain(step, carry):
        cols = pl.ds(pl.multiple_of(step * tn, tn), tn)
        for off in range(1, n_sp):
            other = lax.rem(sp + off, n_sp)
            r_send(step, off).wait_send()
            pltpu.make_async_copy(rs_ref.at[other, :, cols], rs_ref.at[other, :, cols], rrecv.at[step, other]).wait()
        return carry

    lax.fori_loop(0, n_col, drain, 0)
    own_part.wait()
    for off in range(1, n_sp):
        g_send(off).wait_send()
        b_send(off).wait_send()
    for off in range(1, n_dp):
        a_send(off).wait_send()
    for step in range(chips):
        src = hid_ref if step == 0 else None

        @pl.when((chip - step >= 0) & (chip + 1 < chips))
        def _():
            index = (chip - step) * 2 + core
            h_send(index, hid_ref if step == 0 else h_block(index), chip + 1, right_send.at[step]).wait_send()

        @pl.when((chip + step < chips) & (chip >= 1))
        def _():
            index = (chip + step) * 2 + core
            h_send(index, hid_ref if step == 0 else h_block(index), chip - 1, left_send.at[step]).wait_send()

        h_pair(dp, hid_ref, pair_send.at[step]).wait_send()


def exchange(n_dp, n_sp, hidden, d_slot, w_down):
    slots, hid_width = hidden.shape
    slot_rows, width = d_slot.shape
    block = width // n_dp
    tn, th = width // 8, min(256, hid_width)
    n_col = width // tn
    chips = n_dp // 2
    bf = jnp.bfloat16
    dma = pltpu.SemaphoreType.DMA
    hbm = pl.BlockSpec(memory_space=pl.ANY)
    vmem = pl.BlockSpec(memory_space=pltpu.VMEM)
    return pl.pallas_call(
        functools.partial(exchange_kernel, n_dp, n_sp),
        out_shape=(
            jax.ShapeDtypeStruct((n_sp, slot_rows, width), bf),
            jax.ShapeDtypeStruct((slots, hid_width), jnp.float32),
            jax.ShapeDtypeStruct((n_dp, slots, hid_width), bf),
            jax.ShapeDtypeStruct((n_dp, n_sp, slot_rows, block), bf),
        ),
        in_specs=[vmem, vmem, hbm],
        out_specs=(hbm, vmem, hbm, hbm),
        scratch_shapes=[
            pltpu.VMEM((n_sp, slot_rows, width), bf),
            pltpu.VMEM((n_sp, slot_rows, width), bf),
            pltpu.VMEM((2, hid_width, tn), bf),
            pltpu.VMEM((2, th, width), bf),
            dma((4,)),
            dma((4,)),
            dma((chips,)),
            dma((chips,)),
            dma((chips,)),
            dma((n_dp,)),
            dma((n_dp,)),
            dma((n_dp,)),
            dma((n_sp,)),
            dma((n_sp,)),
            dma((n_sp,)),
            dma((n_sp,)),
            dma((n_col, n_sp)),
            dma((n_col, n_sp)),
        ],
        compiler_params=pltpu.CompilerParams(
            collective_id=0, has_side_effects=True, vmem_limit_bytes=60 * 1024 * 1024
        ),
    )(hidden, d_slot, w_down)


def contract_rows(left, right):
    return lax.dot_general(
        left, right, (((0,), (0,)), ((), ())), preferred_element_type=jnp.float32
    )


def local(n_dp, n_sp, gate_pre, up_pre, w_down, route_logits, expert_ids, d_out):
    tok_rows = expert_ids.shape[0]
    slot_rows = tok_rows // 2
    routed = jnp.any(expert_ids == 0, axis=1)
    routed_int = routed.astype(jnp.int32)
    routed_float = routed.astype(jnp.float32)
    slot_rank = jnp.cumsum(routed_int) - 1
    gate_wide = gate_pre.astype(jnp.float32)
    up_wide = up_pre.astype(jnp.float32)
    sigma_gate = jax.nn.sigmoid(gate_wide)
    silu_gate = gate_wide * sigma_gate
    hidden = (silu_gate * up_wide).astype(jnp.bfloat16)
    first_zero = expert_ids[:, 0] == 0
    own_logit = jnp.where(first_zero, route_logits[:, 0], route_logits[:, 1])
    other_logit = jnp.where(first_zero, route_logits[:, 1], route_logits[:, 0])
    weight_zero = routed_float * jax.nn.sigmoid(own_logit - other_logit)
    chooser = (slot_rank[:, None] == jnp.arange(slot_rows, dtype=jnp.int32)[None, :]) & routed[
        :, None
    ]
    picked = contract_rows(chooser.astype(jnp.bfloat16), d_out)
    slot_weight = jnp.sum(jnp.where(chooser, weight_zero[:, None], 0.0), axis=0)
    d_slot = (slot_weight[:, None] * picked).astype(jnp.bfloat16)
    pieces, d_hidden, hidden_all, d_all = exchange(n_dp, n_sp, hidden, d_slot, w_down)
    expert_out = jnp.sum(pieces.astype(jnp.float32), axis=0)
    safe_rank = jnp.clip(slot_rank, 0, slot_rows - 1)
    token_out = expert_out[safe_rank] * routed_float[:, None]
    mixed = (weight_zero[:, None] * token_out).astype(jnp.bfloat16)
    weight_grad = jnp.sum(d_out.astype(jnp.float32) * token_out, axis=1)
    logit_grad = weight_grad * weight_zero * (1.0 - weight_zero)
    first_col = jnp.where(first_zero, logit_grad, -logit_grad)
    logit_grads = jnp.stack([first_col, -first_col], axis=1)
    down_grads = contract_rows(
        hidden_all.reshape(-1, hidden_all.shape[-1]), d_all.reshape(-1, d_all.shape[-1])
    )
    gate_grads = (d_hidden * up_wide * sigma_gate * (1.0 + gate_wide * (1.0 - sigma_gate))).astype(
        jnp.bfloat16
    )
    up_grads = (d_hidden * silu_gate).astype(jnp.bfloat16)
    return (mixed, logit_grads, gate_grads, up_grads, down_grads)


def solution(mesh):
    both = P(("dp", "sp"), None)
    return jax.shard_map(
        functools.partial(local, mesh.shape["dp"], mesh.shape["sp"]),
        mesh=mesh,
        in_specs=(P("dp", "sp"), P("dp", "sp"), P("sp", None), both, both, both),
        out_specs=(both, both, P("dp", "sp"), P("dp", "sp"), P("sp", "dp")),
        check_vma=False,
    )
```

```python
import functools

import jax
import jax.numpy as jnp
from jax import lax
from jax.experimental import pallas as pl
from jax.experimental.pallas import tpu as pltpu
from jax.sharding import PartitionSpec as P

MESH = pl.DeviceIdType.MESH


def exchange_kernel(
    n_dp, n_sp, hid_ref, dslot_ref, w_ref, choose_ref, weight_ref, dout_ref,
    dhid_ref, hall_ref, dall_ref, mixed_ref, wgrad_ref,
    part, rs_ref, dcyc, wcol, wrow, wsem, local_sem,
    right_send, left_send, pair_send, hrecv, asend, arecv, gsend, grecv, bsend, brecv, rsend, rrecv, fsend, frecv,
):
    dp, sp = lax.axis_index("dp"), lax.axis_index("sp")
    chips = n_dp // 2
    chip, core = lax.div(dp, 2), lax.rem(dp, 2)
    slot_rows, width = dslot_ref.shape
    block = width // n_dp
    hid_width = hid_ref.shape[1]
    tn = wcol.shape[2]
    th = wrow.shape[1]
    n_col, n_row = width // tn, hid_width // th

    barrier = pltpu.get_barrier_semaphore()
    for off in range(1, n_dp):
        pl.semaphore_signal(barrier, inc=1, device_id={"dp": lax.rem(dp + off, n_dp)}, device_id_type=MESH)
    for off in range(1, n_sp):
        pl.semaphore_signal(barrier, inc=1, device_id={"sp": lax.rem(sp + off, n_sp)}, device_id_type=MESH)

    def col_load(step, slot):
        return pltpu.make_async_copy(
            w_ref.at[:, pl.ds(pl.multiple_of(step * tn, tn), tn)], wcol.at[slot], wsem.at[slot]
        )

    def row_load(step, slot):
        return pltpu.make_async_copy(
            w_ref.at[pl.ds(pl.multiple_of(step * th, th), th), :], wrow.at[slot], wsem.at[2 + slot]
        )

    col_load(0, 0).start()
    row_load(0, 0).start()
    pl.semaphore_wait(barrier, n_dp - 1 + n_sp - 1)

    def remote(src, dst, send, recv, **where):
        return pltpu.make_async_remote_copy(
            src_ref=src, dst_ref=dst, send_sem=send, recv_sem=recv, device_id=where, device_id_type=MESH
        )

    def a_send(off):
        other = lax.rem(dp + off, n_dp)
        return remote(
            dslot_ref.at[:, pl.ds(pl.multiple_of(other * block, block), block)], dall_ref.at[dp, sp],
            asend.at[off], arecv.at[dp], dp=other,
        )

    def a_wait(off):
        other = lax.rem(dp + off, n_dp)
        pltpu.make_async_copy(dall_ref.at[other, sp], dall_ref.at[other, sp], arecv.at[other]).wait()

    for off in range(1, n_dp):
        a_send(off).start()

    def h_block(index, src=None):
        return hall_ref.at[index]

    def h_send(index, src, to_chip, send):
        return remote(src, hall_ref.at[index], send, hrecv.at[index], dp=to_chip * 2 + core)

    def h_pair(index, src, send):
        return remote(src, hall_ref.at[index], send, hrecv.at[index], dp=chip * 2 + 1 - core)

    def h_wait(index):
        pltpu.make_async_copy(hall_ref.at[index], hall_ref.at[index], hrecv.at[index]).wait()

    @pl.when(chip + 1 < chips)
    def _():
        h_send(dp, hid_ref, chip + 1, right_send.at[0]).start()

    @pl.when(chip >= 1)
    def _():
        h_send(dp, hid_ref, chip - 1, left_send.at[0]).start()

    h_pair(dp, hid_ref, pair_send.at[chip]).start()

    relayed = n_sp == 4
    if relayed:
        near = [sp + 1 - 2 * lax.rem(sp, 2), lax.rem(sp + 2, 4)]
    else:
        near = [lax.rem(sp + off, n_sp) for off in range(1, n_sp)]
    half_rows, half_dp = slot_rows // 2, n_dp // 2

    def g_send(way):
        return remote(dslot_ref, dcyc.at[sp], gsend.at[way], grecv.at[sp], sp=near[way])

    def b_send(way):
        return remote(dall_ref.at[:, sp], dall_ref.at[:, sp], bsend.at[way], brecv.at[sp], sp=near[way])

    def g_half(source, way):
        return dcyc.at[source, way * half_rows:(way + 1) * half_rows]

    def b_half(source, way):
        return dall_ref.at[way * half_dp:(way + 1) * half_dp, source]

    def g_pass(way):
        held = g_half(near[way], way)
        return remote(held, held, fsend.at[way], frecv.at[way], sp=near[1 - way])

    def b_pass(way):
        held = b_half(near[way], way)
        return remote(held, held, fsend.at[2 + way], frecv.at[2 + way], sp=near[1 - way])

    def arrived(ref, sem):
        pltpu.make_async_copy(ref, ref, sem).wait()

    ways = range(len(near))
    for way in ways:
        g_send(way).start()

    own = [
        pltpu.make_async_copy(dslot_ref, dcyc.at[sp], local_sem.at[0]),
        pltpu.make_async_copy(
            dslot_ref.at[:, pl.ds(pl.multiple_of(dp * block, block), block)], dall_ref.at[dp, sp], local_sem.at[1]
        ),
        pltpu.make_async_copy(hid_ref, hall_ref.at[dp], local_sem.at[2]),
    ]
    for copy in own:
        copy.start()

    def r_send(step, off):
        other = lax.rem(sp + off, n_sp)
        cols = pl.ds(pl.multiple_of(step * tn, tn), tn)
        return remote(
            part.at[other, :, cols], rs_ref.at[sp, :, cols],
            rsend.at[step, off], rrecv.at[step, sp], sp=other,
        )

    def col_step(step, carry):
        slot = lax.rem(step, 2)

        @pl.when(step + 1 < n_col)
        def _():
            col_load(step + 1, 1 - slot).start()

        col_load(step, slot).wait()
        cols = pl.ds(pl.multiple_of(step * tn, tn), tn)
        product = jnp.dot(hid_ref[...], wcol[slot], preferred_element_type=jnp.float32)
        part[:, :, cols] = product.astype(jnp.bfloat16).reshape(n_sp, slot_rows, tn)
        for off in range(1, n_sp):
            r_send(step, off).start()
        return carry

    lax.fori_loop(0, n_col, col_step, 0)
    for way in ways:
        arrived(dcyc.at[near[way]], grecv.at[near[way]])
        if relayed:
            g_pass(way).start()

    for copy in own:
        copy.wait()
    for off in range(1, n_dp):
        a_wait(off)

    for way in ways:
        b_send(way).start()

    def relay(step):
        @pl.when(chip - step >= 0)
        def _():
            index = (chip - step) * 2 + core
            h_wait(index)

            @pl.when(chip + 1 < chips)
            def _():
                h_send(index, h_block(index), chip + 1, right_send.at[step]).start()

            h_pair(index, h_block(index), pair_send.at[chip - step]).start()

        @pl.when(chip + step < chips)
        def _():
            index = (chip + step) * 2 + core
            h_wait(index)

            @pl.when(chip >= 1)
            def _():
                h_send(index, h_block(index), chip - 1, left_send.at[step]).start()

            h_pair(index, h_block(index), pair_send.at[chip + step]).start()

    for step in range(1, min(3, chips)):
        relay(step)

    if relayed:
        for way in ways:
            arrived(g_half(3 - sp, way), frecv.at[way])

    def row_step(step, carry):
        slot = lax.rem(step, 2)

        @pl.when(step + 1 < n_row)
        def _():
            row_load(step + 1, 1 - slot).start()

        row_load(step, slot).wait()
        dhid_ref[:, pl.ds(pl.multiple_of(step * th, th), th)] = lax.dot_general(
            dcyc[...].reshape(n_sp * slot_rows, width), wrow[slot], (((1,), (1,)), ((), ())),
            preferred_element_type=jnp.float32,
        )
        return carry

    lax.fori_loop(0, n_row, row_step, 0)

    wgrad_ref[...] = jnp.zeros_like(wgrad_ref)

    def mix_step(step, carry):
        cols = pl.ds(pl.multiple_of(step * tn, tn), tn)
        total = part[sp, :, cols].astype(jnp.float32)
        for off in range(1, n_sp):
            other = lax.rem(sp + off, n_sp)
            arrived(rs_ref.at[other, :, cols], rrecv.at[step, other])
            total = total + rs_ref[other, :, cols].astype(jnp.float32)
        high = total.astype(jnp.bfloat16)
        low = (total - high.astype(jnp.float32)).astype(jnp.bfloat16)
        token_out = jnp.dot(choose_ref[...], high, preferred_element_type=jnp.float32) + jnp.dot(
            choose_ref[...], low, preferred_element_type=jnp.float32
        )
        mixed_ref[:, cols] = (weight_ref[...] * token_out).astype(jnp.bfloat16)
        wgrad_ref[...] += jnp.sum(dout_ref[:, cols].astype(jnp.float32) * token_out, axis=1, keepdims=True)
        for off in range(1, n_sp):
            r_send(step, off).wait_send()
        return carry

    lax.fori_loop(0, n_col, mix_step, 0)

    for way in ways:
        arrived(dall_ref.at[:, near[way]], brecv.at[near[way]])
        if relayed:
            b_pass(way).start()

    for step in range(3, chips):
        relay(step)

    for index in range(chips):
        h_wait(index * 2 + 1 - core)
    for way in ways:
        g_send(way).wait_send()
        b_send(way).wait_send()
        if relayed:
            arrived(b_half(3 - sp, way), frecv.at[2 + way])
            g_pass(way).wait_send()
            b_pass(way).wait_send()
    for off in range(1, n_dp):
        a_send(off).wait_send()
    for step in range(chips):

        @pl.when((chip - step >= 0) & (chip + 1 < chips))
        def _():
            index = (chip - step) * 2 + core
            h_send(index, hid_ref if step == 0 else h_block(index), chip + 1, right_send.at[step]).wait_send()

        @pl.when((chip + step < chips) & (chip >= 1))
        def _():
            index = (chip + step) * 2 + core
            h_send(index, hid_ref if step == 0 else h_block(index), chip - 1, left_send.at[step]).wait_send()

        h_pair(dp, hid_ref, pair_send.at[step]).wait_send()


def exchange(n_dp, n_sp, hidden, d_slot, w_down, choose, weight, d_out):
    slots, hid_width = hidden.shape
    slot_rows, width = d_slot.shape
    block = width // n_dp
    tn, th = width // 8, min(256, hid_width)
    n_col = width // tn
    chips = n_dp // 2
    bf = jnp.bfloat16
    dma = pltpu.SemaphoreType.DMA
    hbm = pl.BlockSpec(memory_space=pl.ANY)
    vmem = pl.BlockSpec(memory_space=pltpu.VMEM)
    return pl.pallas_call(
        functools.partial(exchange_kernel, n_dp, n_sp),
        out_shape=(
            jax.ShapeDtypeStruct((slots, hid_width), jnp.float32),
            jax.ShapeDtypeStruct((n_dp, slots, hid_width), bf),
            jax.ShapeDtypeStruct((n_dp, n_sp, slot_rows, block), bf),
            jax.ShapeDtypeStruct(d_out.shape, bf),
            jax.ShapeDtypeStruct((d_out.shape[0], 1), jnp.float32),
        ),
        in_specs=[vmem, vmem, hbm, vmem, vmem, vmem],
        out_specs=(vmem, hbm, hbm, vmem, vmem),
        scratch_shapes=[
            pltpu.VMEM((n_sp, slot_rows, width), bf),
            pltpu.VMEM((n_sp, slot_rows, width), bf),
            pltpu.VMEM((n_sp, slot_rows, width), bf),
            pltpu.VMEM((2, hid_width, tn), bf),
            pltpu.VMEM((2, th, width), bf),
            dma((4,)),
            dma((4,)),
            dma((chips,)),
            dma((chips,)),
            dma((chips,)),
            dma((n_dp,)),
            dma((n_dp,)),
            dma((n_dp,)),
            dma((n_sp,)),
            dma((n_sp,)),
            dma((n_sp,)),
            dma((n_sp,)),
            dma((n_col, n_sp)),
            dma((n_col, n_sp)),
            dma((4,)),
            dma((4,)),
        ],
        compiler_params=pltpu.CompilerParams(
            collective_id=0, has_side_effects=True, vmem_limit_bytes=60 * 1024 * 1024
        ),
    )(hidden, d_slot, w_down, choose, weight, d_out)


def contract_rows(left, right):
    return lax.dot_general(
        left, right, (((0,), (0,)), ((), ())), preferred_element_type=jnp.float32
    )


def local(n_dp, n_sp, gate_pre, up_pre, w_down, route_logits, expert_ids, d_out):
    tok_rows = expert_ids.shape[0]
    slot_rows = tok_rows // 2
    routed = jnp.any(expert_ids == 0, axis=1)
    routed_int = routed.astype(jnp.int32)
    routed_float = routed.astype(jnp.float32)
    slot_rank = jnp.cumsum(routed_int) - 1
    gate_wide = gate_pre.astype(jnp.float32)
    up_wide = up_pre.astype(jnp.float32)
    sigma_gate = jax.nn.sigmoid(gate_wide)
    silu_gate = gate_wide * sigma_gate
    hidden = (silu_gate * up_wide).astype(jnp.bfloat16)
    first_zero = expert_ids[:, 0] == 0
    own_logit = jnp.where(first_zero, route_logits[:, 0], route_logits[:, 1])
    other_logit = jnp.where(first_zero, route_logits[:, 1], route_logits[:, 0])
    weight_zero = routed_float * jax.nn.sigmoid(own_logit - other_logit)
    chooser = (slot_rank[:, None] == jnp.arange(slot_rows, dtype=jnp.int32)[None, :]) & routed[
        :, None
    ]
    picked = contract_rows(chooser.astype(jnp.bfloat16), d_out)
    slot_weight = jnp.sum(jnp.where(chooser, weight_zero[:, None], 0.0), axis=0)
    d_slot = (slot_weight[:, None] * picked).astype(jnp.bfloat16)
    d_hidden, hidden_all, d_all, mixed, weight_grad = exchange(
        n_dp, n_sp, hidden, d_slot, w_down, chooser.astype(jnp.bfloat16), weight_zero[:, None], d_out
    )
    logit_grad = weight_grad[:, 0] * weight_zero * (1.0 - weight_zero)
    first_col = jnp.where(first_zero, logit_grad, -logit_grad)
    logit_grads = jnp.stack([first_col, -first_col], axis=1)
    down_grads = contract_rows(
        hidden_all.reshape(-1, hidden_all.shape[-1]), d_all.reshape(-1, d_all.shape[-1])
    )
    gate_grads = (d_hidden * up_wide * sigma_gate * (1.0 + gate_wide * (1.0 - sigma_gate))).astype(
        jnp.bfloat16
    )
    up_grads = (d_hidden * silu_gate).astype(jnp.bfloat16)
    return (mixed, logit_grads, gate_grads, up_grads, down_grads)


def solution(mesh):
    both = P(("dp", "sp"), None)
    return jax.shard_map(
        functools.partial(local, mesh.shape["dp"], mesh.shape["sp"]),
        mesh=mesh,
        in_specs=(P("dp", "sp"), P("dp", "sp"), P("sp", None), both, both, both),
        out_specs=(both, both, P("dp", "sp"), P("dp", "sp"), P("sp", "dp")),
        check_vma=False,
    )
```

```python
import functools

import jax
import jax.numpy as jnp
from jax import lax
from jax.experimental import pallas as pl
from jax.experimental.pallas import tpu as pltpu
from jax.sharding import PartitionSpec as P

MESH = pl.DeviceIdType.MESH


def exchange_kernel(
    n_dp, n_sp, hid_ref, dslot_ref, w_ref, choose_ref, weight_ref, dout_ref,
    dhid_ref, hall_ref, dall_ref, mixed_ref, wgrad_ref,
    part, rs_ref, dcyc, wcol, wrow, wsem, local_sem,
    right_send, left_send, pair_send, hrecv, asend, arecv, gsend, grecv, bsend, brecv, rsend, rrecv, fsend, frecv,
):
    dp, sp = lax.axis_index("dp"), lax.axis_index("sp")
    chips = n_dp // 2
    chip, core = lax.div(dp, 2), lax.rem(dp, 2)
    slot_rows, width = dslot_ref.shape
    block = width // n_dp
    hid_width = hid_ref.shape[1]
    tn = wcol.shape[2]
    th = wrow.shape[1]
    n_col, n_row = width // tn, hid_width // th

    barrier = pltpu.get_barrier_semaphore()
    for off in range(1, n_dp):
        pl.semaphore_signal(barrier, inc=1, device_id={"dp": lax.rem(dp + off, n_dp)}, device_id_type=MESH)
    for off in range(1, n_sp):
        pl.semaphore_signal(barrier, inc=1, device_id={"sp": lax.rem(sp + off, n_sp)}, device_id_type=MESH)

    def col_load(step, slot):
        return pltpu.make_async_copy(
            w_ref.at[:, pl.ds(pl.multiple_of(step * tn, tn), tn)], wcol.at[slot], wsem.at[slot]
        )

    def row_load(step, slot):
        return pltpu.make_async_copy(
            w_ref.at[pl.ds(pl.multiple_of(step * th, th), th), :], wrow.at[slot], wsem.at[2 + slot]
        )

    col_load(0, 0).start()
    row_load(0, 0).start()
    pl.semaphore_wait(barrier, n_dp - 1 + n_sp - 1)

    def remote(src, dst, send, recv, **where):
        return pltpu.make_async_remote_copy(
            src_ref=src, dst_ref=dst, send_sem=send, recv_sem=recv, device_id=where, device_id_type=MESH
        )

    def a_send(off):
        other = lax.rem(dp + off, n_dp)
        return remote(
            dslot_ref.at[:, pl.ds(pl.multiple_of(other * block, block), block)], dall_ref.at[dp, sp],
            asend.at[off], arecv.at[dp], dp=other,
        )

    def a_wait(off):
        other = lax.rem(dp + off, n_dp)
        pltpu.make_async_copy(dall_ref.at[other, sp], dall_ref.at[other, sp], arecv.at[other]).wait()

    for off in range(1, n_dp):
        a_send(off).start()

    def h_block(index, src=None):
        return hall_ref.at[index]

    def h_send(index, src, to_chip, send):
        return remote(src, hall_ref.at[index], send, hrecv.at[index], dp=to_chip * 2 + core)

    def h_pair(index, src, send):
        return remote(src, hall_ref.at[index], send, hrecv.at[index], dp=chip * 2 + 1 - core)

    def h_wait(index):
        pltpu.make_async_copy(hall_ref.at[index], hall_ref.at[index], hrecv.at[index]).wait()

    @pl.when(chip + 1 < chips)
    def _():
        h_send(dp, hid_ref, chip + 1, right_send.at[0]).start()

    @pl.when(chip >= 1)
    def _():
        h_send(dp, hid_ref, chip - 1, left_send.at[0]).start()

    h_pair(dp, hid_ref, pair_send.at[chip]).start()

    relayed = n_sp == 4
    if relayed:
        near = [sp + 1 - 2 * lax.rem(sp, 2), lax.rem(sp + 2, 4)]
    else:
        near = [lax.rem(sp + off, n_sp) for off in range(1, n_sp)]
    half_rows, half_dp = slot_rows // 2, n_dp // 2

    def g_send(way):
        return remote(dslot_ref, dcyc.at[sp], gsend.at[way], grecv.at[sp], sp=near[way])

    def b_send(way):
        return remote(dall_ref.at[:, sp], dall_ref.at[:, sp], bsend.at[way], brecv.at[sp], sp=near[way])

    def g_half(source, way):
        return dcyc.at[source, way * half_rows:(way + 1) * half_rows]

    def b_half(source, way):
        return dall_ref.at[way * half_dp:(way + 1) * half_dp, source]

    def g_pass(way):
        held = g_half(near[way], way)
        return remote(held, held, fsend.at[way], frecv.at[way], sp=near[1 - way])

    def b_pass(way):
        held = b_half(near[way], way)
        return remote(held, held, fsend.at[2 + way], frecv.at[2 + way], sp=near[1 - way])

    def arrived(ref, sem):
        pltpu.make_async_copy(ref, ref, sem).wait()

    ways = range(len(near))
    for way in ways:
        g_send(way).start()

    own = [
        pltpu.make_async_copy(dslot_ref, dcyc.at[sp], local_sem.at[0]),
        pltpu.make_async_copy(
            dslot_ref.at[:, pl.ds(pl.multiple_of(dp * block, block), block)], dall_ref.at[dp, sp], local_sem.at[1]
        ),
        pltpu.make_async_copy(hid_ref, hall_ref.at[dp], local_sem.at[2]),
    ]
    for copy in own:
        copy.start()

    def r_send(step, off):
        other = lax.rem(sp + off, n_sp)
        cols = pl.ds(pl.multiple_of(step * tn, tn), tn)
        return remote(
            part.at[other, :, cols], rs_ref.at[sp, :, cols],
            rsend.at[step, off], rrecv.at[step, sp], sp=other,
        )

    def half_cols(step, way):
        half = tn // 2
        return pl.ds(pl.multiple_of(step * tn + way * half, half), half)

    def r_hop(step, way, kind):
        cols = half_cols(step, way)
        src = [part.at[near[way], :, cols], part.at[3 - sp, :, cols], rs_ref.at[3, :, cols]][kind]
        return remote(
            src, rs_ref.at[kind, :, cols], rsend.at[step, 2 * kind + way], rrecv.at[step, 2 * kind + way],
            sp=near[1 - way if kind == 2 else way],
        )

    def r_arrived(step, way, kind):
        arrived(rs_ref.at[kind, :, half_cols(step, way)], rrecv.at[step, 2 * kind + way])

    def fold_step(step, carry):
        for way in range(2):
            cols = half_cols(step, way)
            r_arrived(step, way, 1)
            rs_ref[3, :, cols] = (
                part[near[1 - way], :, cols].astype(jnp.float32) + rs_ref[1, :, cols].astype(jnp.float32)
            ).astype(jnp.bfloat16)
            r_hop(step, way, 2).start()
        return carry

    def col_step(step, carry):
        slot = lax.rem(step, 2)

        @pl.when(step + 1 < n_col)
        def _():
            col_load(step + 1, 1 - slot).start()

        col_load(step, slot).wait()
        cols = pl.ds(pl.multiple_of(step * tn, tn), tn)
        product = jnp.dot(hid_ref[...], wcol[slot], preferred_element_type=jnp.float32)
        part[:, :, cols] = product.astype(jnp.bfloat16).reshape(n_sp, slot_rows, tn)
        if relayed:
            for kind in (1, 0):
                for way in range(2):
                    r_hop(step, way, kind).start()
        else:
            for off in range(1, n_sp):
                r_send(step, off).start()
        return carry

    lax.fori_loop(0, n_col, col_step, 0)
    for way in ways:
        arrived(dcyc.at[near[way]], grecv.at[near[way]])
        if relayed:
            g_pass(way).start()

    for copy in own:
        copy.wait()
    for off in range(1, n_dp):
        a_wait(off)

    for way in ways:
        b_send(way).start()

    def relay(step):
        @pl.when(chip - step >= 0)
        def _():
            index = (chip - step) * 2 + core
            h_wait(index)

            @pl.when(chip + 1 < chips)
            def _():
                h_send(index, h_block(index), chip + 1, right_send.at[step]).start()

            h_pair(index, h_block(index), pair_send.at[chip - step]).start()

        @pl.when(chip + step < chips)
        def _():
            index = (chip + step) * 2 + core
            h_wait(index)

            @pl.when(chip >= 1)
            def _():
                h_send(index, h_block(index), chip - 1, left_send.at[step]).start()

            h_pair(index, h_block(index), pair_send.at[chip + step]).start()

    for step in range(1, min(2, chips)):
        relay(step)

    if relayed:
        lax.fori_loop(0, n_col, fold_step, 0)
        for way in ways:
            arrived(g_half(3 - sp, way), frecv.at[way])

    def row_step(step, carry):
        slot = lax.rem(step, 2)

        @pl.when(step + 1 < n_row)
        def _():
            row_load(step + 1, 1 - slot).start()

        row_load(step, slot).wait()
        dhid_ref[:, pl.ds(pl.multiple_of(step * th, th), th)] = lax.dot_general(
            dcyc[...].reshape(n_sp * slot_rows, width), wrow[slot], (((1,), (1,)), ((), ())),
            preferred_element_type=jnp.float32,
        )
        return carry

    lax.fori_loop(0, n_row, row_step, 0)

    for step in range(2, min(3, chips)):
        relay(step)

    wgrad_ref[...] = jnp.zeros_like(wgrad_ref)

    def mix_step(step, carry):
        cols = pl.ds(pl.multiple_of(step * tn, tn), tn)
        total = part[sp, :, cols].astype(jnp.float32)
        if relayed:
            for kind in (0, 2):
                for way in range(2):
                    r_arrived(step, way, kind)
                total = total + rs_ref[kind, :, cols].astype(jnp.float32)
        else:
            for off in range(1, n_sp):
                other = lax.rem(sp + off, n_sp)
                arrived(rs_ref.at[other, :, cols], rrecv.at[step, other])
                total = total + rs_ref[other, :, cols].astype(jnp.float32)
        high = total.astype(jnp.bfloat16)
        low = (total - high.astype(jnp.float32)).astype(jnp.bfloat16)
        token_out = jnp.dot(choose_ref[...], high, preferred_element_type=jnp.float32) + jnp.dot(
            choose_ref[...], low, preferred_element_type=jnp.float32
        )
        mixed_ref[:, cols] = (weight_ref[...] * token_out).astype(jnp.bfloat16)
        wgrad_ref[...] += jnp.sum(dout_ref[:, cols].astype(jnp.float32) * token_out, axis=1, keepdims=True)
        if relayed:
            for kind in range(3):
                for way in range(2):
                    r_hop(step, way, kind).wait_send()
        else:
            for off in range(1, n_sp):
                r_send(step, off).wait_send()
        return carry

    lax.fori_loop(0, n_col, mix_step, 0)

    for way in ways:
        arrived(dall_ref.at[:, near[way]], brecv.at[near[way]])
        if relayed:
            b_pass(way).start()

    for step in range(3, chips):
        relay(step)

    for index in range(chips):
        h_wait(index * 2 + 1 - core)
    for way in ways:
        g_send(way).wait_send()
        b_send(way).wait_send()
        if relayed:
            arrived(b_half(3 - sp, way), frecv.at[2 + way])
            g_pass(way).wait_send()
            b_pass(way).wait_send()
    for off in range(1, n_dp):
        a_send(off).wait_send()
    for step in range(chips):

        @pl.when((chip - step >= 0) & (chip + 1 < chips))
        def _():
            index = (chip - step) * 2 + core
            h_send(index, hid_ref if step == 0 else h_block(index), chip + 1, right_send.at[step]).wait_send()

        @pl.when((chip + step < chips) & (chip >= 1))
        def _():
            index = (chip + step) * 2 + core
            h_send(index, hid_ref if step == 0 else h_block(index), chip - 1, left_send.at[step]).wait_send()

        h_pair(dp, hid_ref, pair_send.at[step]).wait_send()


def exchange(n_dp, n_sp, hidden, d_slot, w_down, choose, weight, d_out):
    slots, hid_width = hidden.shape
    slot_rows, width = d_slot.shape
    block = width // n_dp
    tn, th = width // 8, min(256, hid_width)
    n_col = width // tn
    chips = n_dp // 2
    bf = jnp.bfloat16
    dma = pltpu.SemaphoreType.DMA
    hbm = pl.BlockSpec(memory_space=pl.ANY)
    vmem = pl.BlockSpec(memory_space=pltpu.VMEM)
    return pl.pallas_call(
        functools.partial(exchange_kernel, n_dp, n_sp),
        out_shape=(
            jax.ShapeDtypeStruct((slots, hid_width), jnp.float32),
            jax.ShapeDtypeStruct((n_dp, slots, hid_width), bf),
            jax.ShapeDtypeStruct((n_dp, n_sp, slot_rows, block), bf),
            jax.ShapeDtypeStruct(d_out.shape, bf),
            jax.ShapeDtypeStruct((d_out.shape[0], 1), jnp.float32),
        ),
        in_specs=[vmem, vmem, hbm, vmem, vmem, vmem],
        out_specs=(vmem, hbm, hbm, vmem, vmem),
        scratch_shapes=[
            pltpu.VMEM((n_sp, slot_rows, width), bf),
            pltpu.VMEM((n_sp, slot_rows, width), bf),
            pltpu.VMEM((n_sp, slot_rows, width), bf),
            pltpu.VMEM((2, hid_width, tn), bf),
            pltpu.VMEM((2, th, width), bf),
            dma((4,)),
            dma((4,)),
            dma((chips,)),
            dma((chips,)),
            dma((chips,)),
            dma((n_dp,)),
            dma((n_dp,)),
            dma((n_dp,)),
            dma((n_sp,)),
            dma((n_sp,)),
            dma((n_sp,)),
            dma((n_sp,)),
            dma((n_col, max(n_sp, 6))),
            dma((n_col, max(n_sp, 6))),
            dma((4,)),
            dma((4,)),
        ],
        compiler_params=pltpu.CompilerParams(
            collective_id=0, has_side_effects=True, vmem_limit_bytes=60 * 1024 * 1024
        ),
    )(hidden, d_slot, w_down, choose, weight, d_out)


def contract_rows(left, right):
    return lax.dot_general(
        left, right, (((0,), (0,)), ((), ())), preferred_element_type=jnp.float32
    )


def local(n_dp, n_sp, gate_pre, up_pre, w_down, route_logits, expert_ids, d_out):
    tok_rows = expert_ids.shape[0]
    slot_rows = tok_rows // 2
    routed = jnp.any(expert_ids == 0, axis=1)
    routed_int = routed.astype(jnp.int32)
    routed_float = routed.astype(jnp.float32)
    slot_rank = jnp.cumsum(routed_int) - 1
    gate_wide = gate_pre.astype(jnp.float32)
    up_wide = up_pre.astype(jnp.float32)
    sigma_gate = jax.nn.sigmoid(gate_wide)
    silu_gate = gate_wide * sigma_gate
    hidden = (silu_gate * up_wide).astype(jnp.bfloat16)
    first_zero = expert_ids[:, 0] == 0
    own_logit = jnp.where(first_zero, route_logits[:, 0], route_logits[:, 1])
    other_logit = jnp.where(first_zero, route_logits[:, 1], route_logits[:, 0])
    weight_zero = routed_float * jax.nn.sigmoid(own_logit - other_logit)
    chooser = (slot_rank[:, None] == jnp.arange(slot_rows, dtype=jnp.int32)[None, :]) & routed[
        :, None
    ]
    picked = contract_rows(chooser.astype(jnp.bfloat16), d_out)
    slot_weight = jnp.sum(jnp.where(chooser, weight_zero[:, None], 0.0), axis=0)
    d_slot = (slot_weight[:, None] * picked).astype(jnp.bfloat16)
    d_hidden, hidden_all, d_all, mixed, weight_grad = exchange(
        n_dp, n_sp, hidden, d_slot, w_down, chooser.astype(jnp.bfloat16), weight_zero[:, None], d_out
    )
    logit_grad = weight_grad[:, 0] * weight_zero * (1.0 - weight_zero)
    first_col = jnp.where(first_zero, logit_grad, -logit_grad)
    logit_grads = jnp.stack([first_col, -first_col], axis=1)
    down_grads = contract_rows(
        hidden_all.reshape(-1, hidden_all.shape[-1]), d_all.reshape(-1, d_all.shape[-1])
    )
    gate_grads = (d_hidden * up_wide * sigma_gate * (1.0 + gate_wide * (1.0 - sigma_gate))).astype(
        jnp.bfloat16
    )
    up_grads = (d_hidden * silu_gate).astype(jnp.bfloat16)
    return (mixed, logit_grads, gate_grads, up_grads, down_grads)


def solution(mesh):
    both = P(("dp", "sp"), None)
    return jax.shard_map(
        functools.partial(local, mesh.shape["dp"], mesh.shape["sp"]),
        mesh=mesh,
        in_specs=(P("dp", "sp"), P("dp", "sp"), P("sp", None), both, both, both),
        out_specs=(both, both, P("dp", "sp"), P("dp", "sp"), P("sp", "dp")),
        check_vma=False,
    )
```

```python
import functools

import jax
import jax.numpy as jnp
from jax import lax
from jax.experimental import pallas as pl
from jax.experimental.pallas import tpu as pltpu
from jax.sharding import PartitionSpec as P

MESH = pl.DeviceIdType.MESH


def exchange_kernel(
    n_dp, n_sp, hid_ref, dslot_ref, w_ref, choose_ref, weight_ref, dout_ref,
    dhid_ref, hall_ref, dall_ref, mixed_ref, wgrad_ref,
    part, rs_ref, dcyc, wcol, wrow, wsem, local_sem,
    right_send, left_send, pair_send, hrecv, asend, arecv, gsend, grecv, bsend, brecv, rsend, rrecv, fsend, frecv,
):
    dp, sp = lax.axis_index("dp"), lax.axis_index("sp")
    chips = n_dp // 2
    chip, core = lax.div(dp, 2), lax.rem(dp, 2)
    slot_rows, width = dslot_ref.shape
    block = width // n_dp
    hid_width = hid_ref.shape[1]
    tn = wcol.shape[2]
    th = wrow.shape[1]
    n_col, n_row = width // tn, hid_width // th

    barrier = pltpu.get_barrier_semaphore()
    for off in range(1, n_dp):
        pl.semaphore_signal(barrier, inc=1, device_id={"dp": lax.rem(dp + off, n_dp)}, device_id_type=MESH)
    for off in range(1, n_sp):
        pl.semaphore_signal(barrier, inc=1, device_id={"sp": lax.rem(sp + off, n_sp)}, device_id_type=MESH)

    def col_load(step, slot):
        return pltpu.make_async_copy(
            w_ref.at[:, pl.ds(pl.multiple_of(step * tn, tn), tn)], wcol.at[slot], wsem.at[slot]
        )

    def row_load(step, slot):
        return pltpu.make_async_copy(
            w_ref.at[pl.ds(pl.multiple_of(step * th, th), th), :], wrow.at[slot], wsem.at[2 + slot]
        )

    col_load(0, 0).start()
    row_load(0, 0).start()
    pl.semaphore_wait(barrier, n_dp - 1 + n_sp - 1)

    def remote(src, dst, send, recv, **where):
        return pltpu.make_async_remote_copy(
            src_ref=src, dst_ref=dst, send_sem=send, recv_sem=recv, device_id=where, device_id_type=MESH
        )

    def a_send(off):
        other = lax.rem(dp + off, n_dp)
        return remote(
            dslot_ref.at[:, pl.ds(pl.multiple_of(other * block, block), block)], dall_ref.at[dp, sp],
            asend.at[off], arecv.at[dp], dp=other,
        )

    def a_wait(off):
        other = lax.rem(dp + off, n_dp)
        pltpu.make_async_copy(dall_ref.at[other, sp], dall_ref.at[other, sp], arecv.at[other]).wait()

    half_slots = hid_ref.shape[0] // 2

    def h_part(index, half):
        return hall_ref.at[index, half * half_slots:(half + 1) * half_slots]

    def own_part(half):
        return hid_ref.at[half * half_slots:(half + 1) * half_slots]

    def h_send(index, half, src, to, send):
        return remote(src, h_part(index, half), send, hrecv.at[2 * index + half], dp=to)

    def h_wait(index, half):
        pltpu.make_async_copy(h_part(index, half), h_part(index, half), hrecv.at[2 * index + half]).wait()

    def h_right(index, half, src, step):
        return h_send(index, half, src, dp + 2, right_send.at[2 * step + half])

    def h_left(index, half, src, step):
        return h_send(index, half, src, dp - 2, left_send.at[2 * step + half])

    def h_pair(index, half, src):
        return h_send(index, half, src, chip * 2 + 1 - core, pair_send.at[2 * lax.div(index, 2) + half])

    for half in range(2):
        @pl.when(chip + 1 < chips)
        def _():
            h_right(dp, half, own_part(half), 0).start()

        @pl.when(chip >= 1)
        def _():
            h_left(dp, half, own_part(half), 0).start()

    for half in range(2):
        h_pair(dp, half, own_part(half)).start()

    for off in range(1, n_dp):
        a_send(off).start()

    relayed = n_sp == 4
    if relayed:
        near = [sp + 1 - 2 * lax.rem(sp, 2), lax.rem(sp + 2, 4)]
    else:
        near = [lax.rem(sp + off, n_sp) for off in range(1, n_sp)]
    half_rows, half_dp = slot_rows // 2, n_dp // 2

    def g_send(way):
        return remote(dslot_ref, dcyc.at[sp], gsend.at[way], grecv.at[sp], sp=near[way])

    def b_send(way):
        return remote(dall_ref.at[:, sp], dall_ref.at[:, sp], bsend.at[way], brecv.at[sp], sp=near[way])

    def g_half(source, way):
        return dcyc.at[source, way * half_rows:(way + 1) * half_rows]

    def b_half(source, way):
        return dall_ref.at[way * half_dp:(way + 1) * half_dp, source]

    def g_pass(way):
        held = g_half(near[way], way)
        return remote(held, held, fsend.at[way], frecv.at[way], sp=near[1 - way])

    def b_pass(way):
        held = b_half(near[way], way)
        return remote(held, held, fsend.at[2 + way], frecv.at[2 + way], sp=near[1 - way])

    def arrived(ref, sem):
        pltpu.make_async_copy(ref, ref, sem).wait()

    ways = range(len(near))
    for way in ways:
        g_send(way).start()

    own = [
        pltpu.make_async_copy(dslot_ref, dcyc.at[sp], local_sem.at[0]),
        pltpu.make_async_copy(
            dslot_ref.at[:, pl.ds(pl.multiple_of(dp * block, block), block)], dall_ref.at[dp, sp], local_sem.at[1]
        ),
        pltpu.make_async_copy(hid_ref, hall_ref.at[dp], local_sem.at[2]),
    ]
    for copy in own:
        copy.start()

    def r_send(step, off):
        other = lax.rem(sp + off, n_sp)
        cols = pl.ds(pl.multiple_of(step * tn, tn), tn)
        return remote(
            part.at[other, :, cols], rs_ref.at[sp, :, cols],
            rsend.at[step, off], rrecv.at[step, sp], sp=other,
        )

    def half_cols(step, way):
        half = tn // 2
        return pl.ds(pl.multiple_of(step * tn + way * half, half), half)

    def r_hop(step, way, kind):
        cols = half_cols(step, way)
        src = [part.at[near[way], :, cols], part.at[3 - sp, :, cols], rs_ref.at[3, :, cols]][kind]
        return remote(
            src, rs_ref.at[kind, :, cols], rsend.at[step, 2 * kind + way], rrecv.at[step, 2 * kind + way],
            sp=near[1 - way if kind == 2 else way],
        )

    def r_arrived(step, way, kind):
        arrived(rs_ref.at[kind, :, half_cols(step, way)], rrecv.at[step, 2 * kind + way])

    def fold_step(step, carry):
        for way in range(2):
            cols = half_cols(step, way)
            r_arrived(step, way, 1)
            rs_ref[3, :, cols] = (
                part[near[1 - way], :, cols].astype(jnp.float32) + rs_ref[1, :, cols].astype(jnp.float32)
            ).astype(jnp.bfloat16)
            r_hop(step, way, 2).start()
        return carry

    def col_step(step, carry):
        slot = lax.rem(step, 2)

        @pl.when(step + 1 < n_col)
        def _():
            col_load(step + 1, 1 - slot).start()

        col_load(step, slot).wait()
        cols = pl.ds(pl.multiple_of(step * tn, tn), tn)
        product = jnp.dot(hid_ref[...], wcol[slot], preferred_element_type=jnp.float32)
        part[:, :, cols] = product.astype(jnp.bfloat16).reshape(n_sp, slot_rows, tn)
        if relayed:
            for kind in (1, 0):
                for way in range(2):
                    r_hop(step, way, kind).start()
        else:
            for off in range(1, n_sp):
                r_send(step, off).start()
        return carry

    lax.fori_loop(0, n_col, col_step, 0)

    def relay(step, half):
        @pl.when(chip - step >= 0)
        def _():
            index = dp - 2 * step
            h_wait(index, half)

            @pl.when(chip + 1 < chips)
            def _():
                h_right(index, half, h_part(index, half), step).start()

            h_pair(index, half, h_part(index, half)).start()

        @pl.when(chip + step < chips)
        def _():
            index = dp + 2 * step
            h_wait(index, half)

            @pl.when(chip >= 1)
            def _():
                h_left(index, half, h_part(index, half), step).start()

            h_pair(index, half, h_part(index, half)).start()

    for way in ways:
        arrived(dcyc.at[near[way]], grecv.at[near[way]])
        if relayed:
            g_pass(way).start()

    if chips > 1:
        for half in range(2):
            relay(1, half)

    if relayed:
        lax.fori_loop(0, n_col, fold_step, 0)

    for copy in own:
        copy.wait()
    for off in range(1, n_dp):
        a_wait(off)

    for way in ways:
        b_send(way).start()

    if relayed:
        for way in ways:
            arrived(g_half(3 - sp, way), frecv.at[way])

    def row_step(step, carry):
        slot = lax.rem(step, 2)

        @pl.when(step + 1 < n_row)
        def _():
            row_load(step + 1, 1 - slot).start()

        row_load(step, slot).wait()
        dhid_ref[:, pl.ds(pl.multiple_of(step * th, th), th)] = lax.dot_general(
            dcyc[...].reshape(n_sp * slot_rows, width), wrow[slot], (((1,), (1,)), ((), ())),
            preferred_element_type=jnp.float32,
        )
        return carry

    for half in range(2):
        lax.fori_loop(half * n_row // 2, (half + 1) * n_row // 2, row_step, 0)
        if chips > 2:
            relay(2, half)

    wgrad_ref[...] = jnp.zeros_like(wgrad_ref)

    def mix_step(step, carry):
        cols = pl.ds(pl.multiple_of(step * tn, tn), tn)
        total = part[sp, :, cols].astype(jnp.float32)
        if relayed:
            for kind in (0, 2):
                for way in range(2):
                    r_arrived(step, way, kind)
                total = total + rs_ref[kind, :, cols].astype(jnp.float32)
        else:
            for off in range(1, n_sp):
                other = lax.rem(sp + off, n_sp)
                arrived(rs_ref.at[other, :, cols], rrecv.at[step, other])
                total = total + rs_ref[other, :, cols].astype(jnp.float32)
        high = total.astype(jnp.bfloat16)
        low = (total - high.astype(jnp.float32)).astype(jnp.bfloat16)
        token_out = jnp.dot(choose_ref[...], high, preferred_element_type=jnp.float32) + jnp.dot(
            choose_ref[...], low, preferred_element_type=jnp.float32
        )
        mixed_ref[:, cols] = (weight_ref[...] * token_out).astype(jnp.bfloat16)
        wgrad_ref[...] += jnp.sum(dout_ref[:, cols].astype(jnp.float32) * token_out, axis=1, keepdims=True)
        if relayed:
            for kind in range(3):
                for way in range(2):
                    r_hop(step, way, kind).wait_send()
        else:
            for off in range(1, n_sp):
                r_send(step, off).wait_send()
        return carry

    lax.fori_loop(0, n_col, mix_step, 0)

    for way in ways:
        arrived(dall_ref.at[:, near[way]], brecv.at[near[way]])
        if relayed:
            b_pass(way).start()

    for step in range(3, chips):
        for half in range(2):
            relay(step, half)

    for index in range(chips):
        for half in range(2):
            h_wait(index * 2 + 1 - core, half)
    for way in ways:
        g_send(way).wait_send()
        b_send(way).wait_send()
        if relayed:
            arrived(b_half(3 - sp, way), frecv.at[2 + way])
            g_pass(way).wait_send()
            b_pass(way).wait_send()
    for off in range(1, n_dp):
        a_send(off).wait_send()
    for step in range(chips):
        for half in range(2):
            @pl.when((chip - step >= 0) & (chip + 1 < chips))
            def _():
                h_right(dp - 2 * step, half, own_part(half), step).wait_send()

            @pl.when((chip + step < chips) & (chip >= 1))
            def _():
                h_left(dp + 2 * step, half, own_part(half), step).wait_send()

            h_send(dp, half, own_part(half), chip * 2 + 1 - core, pair_send.at[2 * step + half]).wait_send()


def exchange(n_dp, n_sp, hidden, d_slot, w_down, choose, weight, d_out):
    slots, hid_width = hidden.shape
    slot_rows, width = d_slot.shape
    block = width // n_dp
    tn, th = width // 8, min(256, hid_width)
    n_col = width // tn
    chips = n_dp // 2
    bf = jnp.bfloat16
    dma = pltpu.SemaphoreType.DMA
    hbm = pl.BlockSpec(memory_space=pl.ANY)
    vmem = pl.BlockSpec(memory_space=pltpu.VMEM)
    return pl.pallas_call(
        functools.partial(exchange_kernel, n_dp, n_sp),
        out_shape=(
            jax.ShapeDtypeStruct((slots, hid_width), jnp.float32),
            jax.ShapeDtypeStruct((n_dp, slots, hid_width), bf),
            jax.ShapeDtypeStruct((n_dp, n_sp, slot_rows, block), bf),
            jax.ShapeDtypeStruct(d_out.shape, bf),
            jax.ShapeDtypeStruct((d_out.shape[0], 1), jnp.float32),
        ),
        in_specs=[vmem, vmem, hbm, vmem, vmem, vmem],
        out_specs=(vmem, hbm, hbm, vmem, vmem),
        scratch_shapes=[
            pltpu.VMEM((n_sp, slot_rows, width), bf),
            pltpu.VMEM((n_sp, slot_rows, width), bf),
            pltpu.VMEM((n_sp, slot_rows, width), bf),
            pltpu.VMEM((2, hid_width, tn), bf),
            pltpu.VMEM((2, th, width), bf),
            dma((4,)),
            dma((4,)),
            dma((2 * chips,)),
            dma((2 * chips,)),
            dma((2 * chips,)),
            dma((2 * n_dp,)),
            dma((n_dp,)),
            dma((n_dp,)),
            dma((n_sp,)),
            dma((n_sp,)),
            dma((n_sp,)),
            dma((n_sp,)),
            dma((n_col, max(n_sp, 6))),
            dma((n_col, max(n_sp, 6))),
            dma((4,)),
            dma((4,)),
        ],
        compiler_params=pltpu.CompilerParams(
            collective_id=0, has_side_effects=True, vmem_limit_bytes=60 * 1024 * 1024
        ),
    )(hidden, d_slot, w_down, choose, weight, d_out)


def contract_rows(left, right):
    return lax.dot_general(
        left, right, (((0,), (0,)), ((), ())), preferred_element_type=jnp.float32
    )


def local(n_dp, n_sp, gate_pre, up_pre, w_down, route_logits, expert_ids, d_out):
    tok_rows = expert_ids.shape[0]
    slot_rows = tok_rows // 2
    routed = jnp.any(expert_ids == 0, axis=1)
    routed_int = routed.astype(jnp.int32)
    routed_float = routed.astype(jnp.float32)
    slot_rank = jnp.cumsum(routed_int) - 1
    gate_wide = gate_pre.astype(jnp.float32)
    up_wide = up_pre.astype(jnp.float32)
    sigma_gate = jax.nn.sigmoid(gate_wide)
    silu_gate = gate_wide * sigma_gate
    hidden = (silu_gate * up_wide).astype(jnp.bfloat16)
    first_zero = expert_ids[:, 0] == 0
    own_logit = jnp.where(first_zero, route_logits[:, 0], route_logits[:, 1])
    other_logit = jnp.where(first_zero, route_logits[:, 1], route_logits[:, 0])
    weight_zero = routed_float * jax.nn.sigmoid(own_logit - other_logit)
    chooser = (slot_rank[:, None] == jnp.arange(slot_rows, dtype=jnp.int32)[None, :]) & routed[
        :, None
    ]
    picked = contract_rows(chooser.astype(jnp.bfloat16), d_out)
    slot_weight = jnp.sum(jnp.where(chooser, weight_zero[:, None], 0.0), axis=0)
    d_slot = (slot_weight[:, None] * picked).astype(jnp.bfloat16)
    d_hidden, hidden_all, d_all, mixed, weight_grad = exchange(
        n_dp, n_sp, hidden, d_slot, w_down, chooser.astype(jnp.bfloat16), weight_zero[:, None], d_out
    )
    logit_grad = weight_grad[:, 0] * weight_zero * (1.0 - weight_zero)
    first_col = jnp.where(first_zero, logit_grad, -logit_grad)
    logit_grads = jnp.stack([first_col, -first_col], axis=1)
    down_grads = contract_rows(
        hidden_all.reshape(-1, hidden_all.shape[-1]), d_all.reshape(-1, d_all.shape[-1])
    )
    gate_grads = (d_hidden * up_wide * sigma_gate * (1.0 + gate_wide * (1.0 - sigma_gate))).astype(
        jnp.bfloat16
    )
    up_grads = (d_hidden * silu_gate).astype(jnp.bfloat16)
    return (mixed, logit_grads, gate_grads, up_grads, down_grads)


def solution(mesh):
    both = P(("dp", "sp"), None)
    return jax.shard_map(
        functools.partial(local, mesh.shape["dp"], mesh.shape["sp"]),
        mesh=mesh,
        in_specs=(P("dp", "sp"), P("dp", "sp"), P("sp", None), both, both, both),
        out_specs=(both, both, P("dp", "sp"), P("dp", "sp"), P("sp", "dp")),
        check_vma=False,
    )
```

```python
import functools

import jax
import jax.numpy as jnp
from jax import lax
from jax.experimental import pallas as pl
from jax.experimental.pallas import tpu as pltpu
from jax.sharding import PartitionSpec as P

MESH = pl.DeviceIdType.MESH


def exchange_kernel(
    n_dp, n_sp, hid_ref, slot_choose_ref, slot_weight_ref, w_ref, choose_ref, weight_ref, dout_ref,
    dhid_ref, hall_ref, dall_ref, mixed_ref, wgrad_ref,
    dslot_ref, part, rs_ref, dcyc, wcol, wrow, wsem, local_sem,
    right_send, left_send, pair_send, hrecv, asend, arecv, gsend, grecv, bsend, brecv, rsend, rrecv, fsend, frecv,
):
    dp, sp = lax.axis_index("dp"), lax.axis_index("sp")
    chips = n_dp // 2
    chip, core = lax.div(dp, 2), lax.rem(dp, 2)
    slot_rows, width = dslot_ref.shape
    block = width // n_dp
    hid_width = hid_ref.shape[1]
    tn = wcol.shape[2]
    th = wrow.shape[1]
    n_col, n_row = width // tn, hid_width // th

    barrier = pltpu.get_barrier_semaphore()
    for off in range(1, n_dp):
        pl.semaphore_signal(barrier, inc=1, device_id={"dp": lax.rem(dp + off, n_dp)}, device_id_type=MESH)
    for off in range(1, n_sp):
        pl.semaphore_signal(barrier, inc=1, device_id={"sp": lax.rem(sp + off, n_sp)}, device_id_type=MESH)

    def col_load(step, slot):
        return pltpu.make_async_copy(
            w_ref.at[:, pl.ds(pl.multiple_of(step * tn, tn), tn)], wcol.at[slot], wsem.at[slot]
        )

    def row_load(step, slot):
        return pltpu.make_async_copy(
            w_ref.at[pl.ds(pl.multiple_of(step * th, th), th), :], wrow.at[slot], wsem.at[2 + slot]
        )

    col_load(0, 0).start()
    row_load(0, 0).start()
    pl.semaphore_wait(barrier, n_dp - 1 + n_sp - 1)

    def remote(src, dst, send, recv, **where):
        return pltpu.make_async_remote_copy(
            src_ref=src, dst_ref=dst, send_sem=send, recv_sem=recv, device_id=where, device_id_type=MESH
        )

    def a_send(off):
        other = lax.rem(dp + off, n_dp)
        return remote(
            dslot_ref.at[:, pl.ds(pl.multiple_of(other * block, block), block)], dall_ref.at[dp, sp],
            asend.at[off], arecv.at[dp], dp=other,
        )

    def a_wait(off):
        other = lax.rem(dp + off, n_dp)
        pltpu.make_async_copy(dall_ref.at[other, sp], dall_ref.at[other, sp], arecv.at[other]).wait()

    half_slots = hid_ref.shape[0] // 2

    def h_part(index, half):
        return hall_ref.at[index, half * half_slots:(half + 1) * half_slots]

    def own_part(half):
        return hid_ref.at[half * half_slots:(half + 1) * half_slots]

    def h_send(index, half, src, to, send):
        return remote(src, h_part(index, half), send, hrecv.at[2 * index + half], dp=to)

    def h_wait(index, half):
        pltpu.make_async_copy(h_part(index, half), h_part(index, half), hrecv.at[2 * index + half]).wait()

    def h_right(index, half, src, step):
        return h_send(index, half, src, dp + 2, right_send.at[2 * step + half])

    def h_left(index, half, src, step):
        return h_send(index, half, src, dp - 2, left_send.at[2 * step + half])

    def h_pair(index, half, src):
        return h_send(index, half, src, chip * 2 + 1 - core, pair_send.at[2 * lax.div(index, 2) + half])

    for half in range(2):
        @pl.when(chip + 1 < chips)
        def _():
            h_right(dp, half, own_part(half), 0).start()

        @pl.when(chip >= 1)
        def _():
            h_left(dp, half, own_part(half), 0).start()

    for half in range(2):
        h_pair(dp, half, own_part(half)).start()

    def slot_step(step, carry):
        cols = pl.ds(pl.multiple_of(step * tn, tn), tn)
        picked = jnp.dot(slot_choose_ref[...], dout_ref[:, cols], preferred_element_type=jnp.float32)
        dslot_ref[:, cols] = (slot_weight_ref[...] * picked).astype(jnp.bfloat16)
        return carry

    lax.fori_loop(0, n_col, slot_step, 0)

    for off in range(1, n_dp):
        a_send(off).start()

    relayed = n_sp == 4
    if relayed:
        near = [sp + 1 - 2 * lax.rem(sp, 2), lax.rem(sp + 2, 4)]
    else:
        near = [lax.rem(sp + off, n_sp) for off in range(1, n_sp)]
    half_rows, half_dp = slot_rows // 2, n_dp // 2

    def g_send(way):
        return remote(dslot_ref, dcyc.at[sp], gsend.at[way], grecv.at[sp], sp=near[way])

    def b_send(way):
        return remote(dall_ref.at[:, sp], dall_ref.at[:, sp], bsend.at[way], brecv.at[sp], sp=near[way])

    def g_half(source, way):
        return dcyc.at[source, way * half_rows:(way + 1) * half_rows]

    def b_half(source, way):
        return dall_ref.at[way * half_dp:(way + 1) * half_dp, source]

    def g_pass(way):
        held = g_half(near[way], way)
        return remote(held, held, fsend.at[way], frecv.at[way], sp=near[1 - way])

    def b_pass(way):
        held = b_half(near[way], way)
        return remote(held, held, fsend.at[2 + way], frecv.at[2 + way], sp=near[1 - way])

    def arrived(ref, sem):
        pltpu.make_async_copy(ref, ref, sem).wait()

    ways = range(len(near))
    for way in ways:
        g_send(way).start()

    own = [
        pltpu.make_async_copy(dslot_ref, dcyc.at[sp], local_sem.at[0]),
        pltpu.make_async_copy(
            dslot_ref.at[:, pl.ds(pl.multiple_of(dp * block, block), block)], dall_ref.at[dp, sp], local_sem.at[1]
        ),
        pltpu.make_async_copy(hid_ref, hall_ref.at[dp], local_sem.at[2]),
    ]
    for copy in own:
        copy.start()

    def r_send(step, off):
        other = lax.rem(sp + off, n_sp)
        cols = pl.ds(pl.multiple_of(step * tn, tn), tn)
        return remote(
            part.at[other, :, cols], rs_ref.at[sp, :, cols],
            rsend.at[step, off], rrecv.at[step, sp], sp=other,
        )

    def half_cols(step, way):
        half = tn // 2
        return pl.ds(pl.multiple_of(step * tn + way * half, half), half)

    def r_hop(step, way, kind):
        cols = half_cols(step, way)
        src = [part.at[near[way], :, cols], part.at[3 - sp, :, cols], rs_ref.at[3, :, cols]][kind]
        return remote(
            src, rs_ref.at[kind, :, cols], rsend.at[step, 2 * kind + way], rrecv.at[step, 2 * kind + way],
            sp=near[1 - way if kind == 2 else way],
        )

    def r_arrived(step, way, kind):
        arrived(rs_ref.at[kind, :, half_cols(step, way)], rrecv.at[step, 2 * kind + way])

    def fold_step(step, carry):
        for way in range(2):
            cols = half_cols(step, way)
            r_arrived(step, way, 1)
            rs_ref[3, :, cols] = (
                part[near[1 - way], :, cols].astype(jnp.float32) + rs_ref[1, :, cols].astype(jnp.float32)
            ).astype(jnp.bfloat16)
            r_hop(step, way, 2).start()
        return carry

    def col_step(step, carry):
        slot = lax.rem(step, 2)

        @pl.when(step + 1 < n_col)
        def _():
            col_load(step + 1, 1 - slot).start()

        col_load(step, slot).wait()
        cols = pl.ds(pl.multiple_of(step * tn, tn), tn)
        product = jnp.dot(hid_ref[...], wcol[slot], preferred_element_type=jnp.float32)
        part[:, :, cols] = product.astype(jnp.bfloat16).reshape(n_sp, slot_rows, tn)
        if relayed:
            for kind in (1, 0):
                for way in range(2):
                    r_hop(step, way, kind).start()
        else:
            for off in range(1, n_sp):
                r_send(step, off).start()
        return carry

    lax.fori_loop(0, n_col, col_step, 0)

    def relay(step, half):
        @pl.when(chip - step >= 0)
        def _():
            index = dp - 2 * step
            h_wait(index, half)

            @pl.when(chip + 1 < chips)
            def _():
                h_right(index, half, h_part(index, half), step).start()

            h_pair(index, half, h_part(index, half)).start()

        @pl.when(chip + step < chips)
        def _():
            index = dp + 2 * step
            h_wait(index, half)

            @pl.when(chip >= 1)
            def _():
                h_left(index, half, h_part(index, half), step).start()

            h_pair(index, half, h_part(index, half)).start()

    for way in ways:
        arrived(dcyc.at[near[way]], grecv.at[near[way]])
        if relayed:
            g_pass(way).start()

    if chips > 1:
        for half in range(2):
            relay(1, half)

    if relayed:
        lax.fori_loop(0, n_col, fold_step, 0)

    for copy in own:
        copy.wait()
    for off in range(1, n_dp):
        a_wait(off)

    for way in ways:
        b_send(way).start()

    if relayed:
        for way in ways:
            arrived(g_half(3 - sp, way), frecv.at[way])

    def row_step(step, carry):
        slot = lax.rem(step, 2)

        @pl.when(step + 1 < n_row)
        def _():
            row_load(step + 1, 1 - slot).start()

        row_load(step, slot).wait()
        dhid_ref[:, pl.ds(pl.multiple_of(step * th, th), th)] = lax.dot_general(
            dcyc[...].reshape(n_sp * slot_rows, width), wrow[slot], (((1,), (1,)), ((), ())),
            preferred_element_type=jnp.float32,
        )
        return carry

    for half in range(2):
        lax.fori_loop(half * n_row // 2, (half + 1) * n_row // 2, row_step, 0)
        if chips > 2:
            relay(2, half)

    wgrad_ref[...] = jnp.zeros_like(wgrad_ref)

    def mix_step(step, carry):
        cols = pl.ds(pl.multiple_of(step * tn, tn), tn)
        total = part[sp, :, cols].astype(jnp.float32)
        if relayed:
            for kind in (0, 2):
                for way in range(2):
                    r_arrived(step, way, kind)
                total = total + rs_ref[kind, :, cols].astype(jnp.float32)
        else:
            for off in range(1, n_sp):
                other = lax.rem(sp + off, n_sp)
                arrived(rs_ref.at[other, :, cols], rrecv.at[step, other])
                total = total + rs_ref[other, :, cols].astype(jnp.float32)
        high = total.astype(jnp.bfloat16)
        low = (total - high.astype(jnp.float32)).astype(jnp.bfloat16)
        token_out = jnp.dot(choose_ref[...], high, preferred_element_type=jnp.float32) + jnp.dot(
            choose_ref[...], low, preferred_element_type=jnp.float32
        )
        mixed_ref[:, cols] = (weight_ref[...] * token_out).astype(jnp.bfloat16)
        wgrad_ref[...] += jnp.sum(dout_ref[:, cols].astype(jnp.float32) * token_out, axis=1, keepdims=True)
        if relayed:
            for kind in range(3):
                for way in range(2):
                    r_hop(step, way, kind).wait_send()
        else:
            for off in range(1, n_sp):
                r_send(step, off).wait_send()
        return carry

    lax.fori_loop(0, n_col, mix_step, 0)

    for way in ways:
        arrived(dall_ref.at[:, near[way]], brecv.at[near[way]])
        if relayed:
            b_pass(way).start()

    for step in range(3, chips):
        for half in range(2):
            relay(step, half)

    for index in range(chips):
        for half in range(2):
            h_wait(index * 2 + 1 - core, half)
    for way in ways:
        g_send(way).wait_send()
        b_send(way).wait_send()
        if relayed:
            arrived(b_half(3 - sp, way), frecv.at[2 + way])
            g_pass(way).wait_send()
            b_pass(way).wait_send()
    for off in range(1, n_dp):
        a_send(off).wait_send()
    for step in range(chips):
        for half in range(2):
            @pl.when((chip - step >= 0) & (chip + 1 < chips))
            def _():
                h_right(dp - 2 * step, half, own_part(half), step).wait_send()

            @pl.when((chip + step < chips) & (chip >= 1))
            def _():
                h_left(dp + 2 * step, half, own_part(half), step).wait_send()

            h_send(dp, half, own_part(half), chip * 2 + 1 - core, pair_send.at[2 * step + half]).wait_send()


def exchange(n_dp, n_sp, hidden, slot_choose, slot_weight, w_down, choose, weight, d_out):
    slots, hid_width = hidden.shape
    slot_rows, width = slot_choose.shape[0], d_out.shape[1]
    block = width // n_dp
    tn, th = width // 8, min(256, hid_width)
    n_col = width // tn
    chips = n_dp // 2
    bf = jnp.bfloat16
    dma = pltpu.SemaphoreType.DMA
    hbm = pl.BlockSpec(memory_space=pl.ANY)
    vmem = pl.BlockSpec(memory_space=pltpu.VMEM)
    return pl.pallas_call(
        functools.partial(exchange_kernel, n_dp, n_sp),
        out_shape=(
            jax.ShapeDtypeStruct((slots, hid_width), jnp.float32),
            jax.ShapeDtypeStruct((n_dp, slots, hid_width), bf),
            jax.ShapeDtypeStruct((n_dp, n_sp, slot_rows, block), bf),
            jax.ShapeDtypeStruct(d_out.shape, bf),
            jax.ShapeDtypeStruct((d_out.shape[0], 1), jnp.float32),
        ),
        in_specs=[vmem, vmem, vmem, hbm, vmem, vmem, vmem],
        out_specs=(vmem, hbm, hbm, vmem, vmem),
        scratch_shapes=[
            pltpu.VMEM((slot_rows, width), bf),
            pltpu.VMEM((n_sp, slot_rows, width), bf),
            pltpu.VMEM((n_sp, slot_rows, width), bf),
            pltpu.VMEM((n_sp, slot_rows, width), bf),
            pltpu.VMEM((2, hid_width, tn), bf),
            pltpu.VMEM((2, th, width), bf),
            dma((4,)),
            dma((4,)),
            dma((2 * chips,)),
            dma((2 * chips,)),
            dma((2 * chips,)),
            dma((2 * n_dp,)),
            dma((n_dp,)),
            dma((n_dp,)),
            dma((n_sp,)),
            dma((n_sp,)),
            dma((n_sp,)),
            dma((n_sp,)),
            dma((n_col, max(n_sp, 6))),
            dma((n_col, max(n_sp, 6))),
            dma((4,)),
            dma((4,)),
        ],
        compiler_params=pltpu.CompilerParams(
            collective_id=0, has_side_effects=True, vmem_limit_bytes=60 * 1024 * 1024
        ),
    )(hidden, slot_choose, slot_weight, w_down, choose, weight, d_out)


def contract_rows(left, right):
    return lax.dot_general(
        left, right, (((0,), (0,)), ((), ())), preferred_element_type=jnp.float32
    )


def local(n_dp, n_sp, gate_pre, up_pre, w_down, route_logits, expert_ids, d_out):
    tok_rows = expert_ids.shape[0]
    slot_rows = tok_rows // 2
    routed = jnp.any(expert_ids == 0, axis=1)
    routed_int = routed.astype(jnp.int32)
    routed_float = routed.astype(jnp.float32)
    slot_rank = jnp.cumsum(routed_int) - 1
    gate_wide = gate_pre.astype(jnp.float32)
    up_wide = up_pre.astype(jnp.float32)
    sigma_gate = jax.nn.sigmoid(gate_wide)
    silu_gate = gate_wide * sigma_gate
    hidden = (silu_gate * up_wide).astype(jnp.bfloat16)
    first_zero = expert_ids[:, 0] == 0
    own_logit = jnp.where(first_zero, route_logits[:, 0], route_logits[:, 1])
    other_logit = jnp.where(first_zero, route_logits[:, 1], route_logits[:, 0])
    weight_zero = routed_float * jax.nn.sigmoid(own_logit - other_logit)
    chooser = (slot_rank[:, None] == jnp.arange(slot_rows, dtype=jnp.int32)[None, :]) & routed[
        :, None
    ]
    slot_weight = jnp.sum(jnp.where(chooser, weight_zero[:, None], 0.0), axis=0)
    d_hidden, hidden_all, d_all, mixed, weight_grad = exchange(
        n_dp, n_sp, hidden, chooser.T.astype(jnp.bfloat16), slot_weight[:, None], w_down, chooser.astype(jnp.bfloat16), weight_zero[:, None], d_out
    )
    logit_grad = weight_grad[:, 0] * weight_zero * (1.0 - weight_zero)
    first_col = jnp.where(first_zero, logit_grad, -logit_grad)
    logit_grads = jnp.stack([first_col, -first_col], axis=1)
    down_grads = contract_rows(
        hidden_all.reshape(-1, hidden_all.shape[-1]), d_all.reshape(-1, d_all.shape[-1])
    )
    gate_grads = (d_hidden * up_wide * sigma_gate * (1.0 + gate_wide * (1.0 - sigma_gate))).astype(
        jnp.bfloat16
    )
    up_grads = (d_hidden * silu_gate).astype(jnp.bfloat16)
    return (mixed, logit_grads, gate_grads, up_grads, down_grads)


def solution(mesh):
    both = P(("dp", "sp"), None)
    return jax.shard_map(
        functools.partial(local, mesh.shape["dp"], mesh.shape["sp"]),
        mesh=mesh,
        in_specs=(P("dp", "sp"), P("dp", "sp"), P("sp", None), both, both, both),
        out_specs=(both, both, P("dp", "sp"), P("dp", "sp"), P("sp", "dp")),
        check_vma=False,
    )
```
